32 devices in a mesh: clips: 2 (over y), frame: 4 (over z), row: 2 (over x), head: 2 (over core).
Axes of the slice: x: 2, y: 2, z: 4, core: 2. Of those that a mesh axis runs over, the one named last changes fastest.
Arguments:
- query: bfloat16 [64, 16, 8, 1536], P(('clips', 'frame'), 'row', None, 'head'), parts along dimension 0, may hold values from -7 to 7
- keys: bfloat16 [64, 16, 8, 1536], P(('clips', 'frame'), 'row', None, 'head'), parts along dimension 0, may hold values from -6 to 6
- values: bfloat16 [64, 16, 8, 1536], P(('clips', 'frame'), 'row', None, 'head'), parts along dimension 0, may hold values from -6 to 6
Outputs:
- attended: bfloat16 [64, 16, 8, 1536], P(('clips', 'frame'), 'row', None, 'head'), parts along dimension 0
The draws below stay inside these ranges and needn't reach their ends.
There are 2 independent parts, one for each index of `clips`. The reference program is written for one: setup_inputs(seed, part) draws one part's arguments, and reference() takes and returns one part's arrays. A program takes and returns all parts, laid end to end along the dimension named above; each array names one. Nothing has to cross between parts.
All inputs are finite; a program needn't handle non-finite values.
Results may differ from the reference program's by a relative error of at most 0.0047.
Values may be sent and summed in bfloat16 or wider, within the bound.
A program may use at most 64 MiB of HBM per device.

```python
import math
import jax
import jax.numpy as jnp
from jax import lax

HEADS = 12
HD = 128
TF = 4
TR = 8
TC = 8
LATENT_FRAMES = 32
ROWS = 16
COLS = 8


def draw_query(key, part):
    full_shape = (LATENT_FRAMES, ROWS, COLS, HEADS * HD)
    result_values = jnp.clip(jax.random.normal(jax.random.fold_in(key, 21), full_shape, jnp.float32), -6.0, 6.0)
    return result_values.astype(jnp.bfloat16)


def draw_keys(key, part):
    full_shape = (LATENT_FRAMES, ROWS, COLS, HEADS * HD)
    result_values = jnp.clip(jax.random.normal(jax.random.fold_in(key, 31), full_shape, jnp.float32), -6.0, 6.0)
    return result_values.astype(jnp.bfloat16)


def shard_levels(own_key, shape, split, least, largest):
    loudness = 1.0
    for dim, parts in split:
        heights = jax.random.uniform(jax.random.fold_in(jax.random.fold_in(own_key, 6), dim), (parts,), jnp.float32, least / len(split), largest / len(split))
        loudness = loudness * jnp.repeat(jnp.exp(heights), shape[dim] // parts).reshape((-1,) + (1,) * (len(shape) - 1 - dim))
    return loudness


def noise(own_key, extent, width, bound, shards=(), kind=jnp.bfloat16):
    values = jax.random.normal(own_key, extent, jnp.float32) * width
    if len(shards) > 0:
        values = shard_levels(own_key, extent, shards, -0.22, 0.18) * values
    return jnp.clip(values, min=-bound, max=bound).astype(kind)


def setup_inputs(seed: int = 0, part: int = 0) -> dict:
    arg_keys = jax.random.split(jax.random.key(seed), 4)
    part_splits = jax.random.split(jax.random.fold_in(arg_keys[3], part), 4)
    return {
        "query": draw_query(jax.random.fold_in(jax.random.fold_in(arg_keys[3], part), 71), part),
        "keys": draw_keys(jax.random.fold_in(jax.random.fold_in(arg_keys[3], part), 71), part),
        "values": noise(part_splits[2], (LATENT_FRAMES, ROWS, COLS, HEADS * HD), 1.0, 6.0, ((0, 4), (1, 2), (3, 2))),
    }


def reference(query, keys, values):
    frames, rows, columns, features = query.shape
    heads = features // HD
    frame_tiles = frames // TF
    row_tiles = rows // TR
    column_tiles = columns // TC
    tile_size = TF * TR * TC
    score_scale = 1.0 / math.sqrt(HD)

    def tiled(array):
        shaped = array.reshape(frame_tiles, TF, row_tiles, TR, column_tiles, TC, heads, HD)
        shaped = shaped.transpose(0, 2, 4, 1, 3, 5, 6, 7)
        return shaped.reshape(frame_tiles, row_tiles, column_tiles, tile_size, heads, HD)
    padding = ((1, 1), (1, 1), (0, 0), (0, 0), (0, 0), (0, 0))
    tiled_queries = tiled(query)
    key_tiles = jnp.pad(tiled(keys), padding)
    value_tiles = jnp.pad(tiled(values), padding)
    offsets = jnp.arange(3, dtype=jnp.int32) - 1
    block_rows = column_tiles * tile_size

    def one_tile(flat):
        frame_at = (flat // row_tiles).astype(jnp.int32)
        row_at = (flat % row_tiles).astype(jnp.int32)
        zero = jnp.zeros((), jnp.int32)
        starts = (frame_at, row_at, zero, zero, zero, zero)
        query_block = lax.dynamic_slice(tiled_queries, starts, (1, 1, column_tiles, tile_size, heads, HD))
        key_block = lax.dynamic_slice(key_tiles, starts, (3, 3, column_tiles, tile_size, heads, HD))
        value_block = lax.dynamic_slice(value_tiles, starts, (3, 3, column_tiles, tile_size, heads, HD))
        frame_ids = frame_at + offsets
        row_ids = row_at + offsets
        frame_ok = (frame_ids >= 0) & (frame_ids < frame_tiles)
        row_ok = (row_ids >= 0) & (row_ids < row_tiles)
        tile_mask = frame_ok[:, None] & row_ok[None, :]
        allowed = jnp.broadcast_to(tile_mask[None, :, :, None], (block_rows, 3, 3, block_rows))
        allowed = allowed.reshape(block_rows, 9 * block_rows)
        queries = query_block.reshape(block_rows, heads, HD).astype(jnp.float32)
        key_rows = key_block.reshape(-1, heads, HD).astype(jnp.float32)
        value_rows = value_block.reshape(-1, heads, HD).astype(jnp.float32)
        scores = jnp.einsum('qhd,khd->hqk', queries, key_rows) * score_scale
        scores = jnp.where(allowed[None], scores, -jnp.inf)
        row_peak = lax.optimization_barrier(jnp.max(scores, axis=-1, keepdims=True))
        weights = jnp.exp(scores - row_peak)
        row_total = lax.optimization_barrier(jnp.sum(weights, axis=-1, keepdims=True))
        rounded_length = lax.optimization_barrier(weights.astype(jnp.bfloat16)).astype(jnp.float32)
        summed = jnp.einsum('hqk,khd->qhd', rounded_length, value_rows)
        return (summed / jnp.transpose(row_total, (1, 0, 2))).astype(jnp.bfloat16)
    results = lax.map(one_tile, jnp.arange(frame_tiles * row_tiles, dtype=jnp.int32))
    results = results.reshape(frame_tiles, row_tiles, column_tiles, TF, TR, TC, heads, HD)
    results = results.transpose(0, 3, 1, 4, 2, 5, 6, 7)
    return results.reshape(frames, rows, columns, features)
```

```python
import functools
import math

import jax
import jax.numpy as jnp
from jax import lax
from jax.experimental import pallas as pl
from jax.experimental.pallas import tpu as pltpu
from jax.sharding import PartitionSpec as P

HD = 128
TF = 4
TR = 8
TC = 8


def shift(cells, axis, forward):
    count = lax.axis_size(axis)
    if forward:
        pairs = [(i, i + 1) for i in range(count - 1)]
    else:
        pairs = [(i + 1, i) for i in range(count - 1)]
    return lax.ppermute(cells, axis, pairs)


def attention_kernel(bias_ref, q_ref, k_ref, v_ref, o_ref, *, tile_frames, score_scale):
    for j in range(tile_frames):
        q = q_ref[j]
        k = k_ref[:, j : j + 3].reshape(-1, HD)
        v = v_ref[:, j : j + 3].reshape(-1, HD)
        s = lax.dot_general(q, k, (((1,), (1,)), ((), ())), preferred_element_type=jnp.float32)
        s = s * score_scale + bias_ref[j]
        m = jnp.max(s, axis=1, keepdims=True)
        p = jnp.exp(s - m)
        l = jnp.sum(p, axis=1, keepdims=True)
        o = jnp.dot(p.astype(jnp.bfloat16), v, preferred_element_type=jnp.float32)
        o_ref[j] = (o / l).astype(o_ref.dtype)


def per_device(query, keys, values):
    frames, rows, columns, features = query.shape
    tile_frames = frames // TF
    tile_size = TF * TR * TC
    heads_here = features // HD
    score_scale = 1.0 / math.sqrt(HD)

    def tiles(x):
        return x.reshape(tile_frames, tile_size, features)

    kv = (tiles(keys), tiles(values))
    above = shift(kv, "row", True)
    below = shift(kv, "row", False)
    own_prev = shift(tuple(x[tile_frames - 1] for x in kv), "frame", True)
    own_next = shift(tuple(x[0] for x in kv), "frame", False)
    diag_prev = shift(
        tuple(jnp.stack((a[tile_frames - 1], b[tile_frames - 1])) for a, b in zip(above, below)),
        "frame",
        True,
    )
    diag_next = shift(tuple(jnp.stack((a[0], b[0])) for a, b in zip(above, below)), "frame", False)

    def window(i):
        middle = jnp.concatenate((own_prev[i][None], kv[i], own_next[i][None]), 0)
        top = jnp.concatenate((diag_prev[i][0][None], above[i], diag_next[i][0][None]), 0)
        bottom = jnp.concatenate((diag_prev[i][1][None], below[i], diag_next[i][1][None]), 0)
        return jnp.stack((top, middle, bottom))

    key_window = window(0)
    value_window = window(1)

    frame_index = lax.axis_index("frame")
    row_index = lax.axis_index("row")
    offsets = jnp.arange(3, dtype=jnp.int32) - 1
    global_frames = frame_index * tile_frames + jnp.arange(tile_frames + 2, dtype=jnp.int32) - 1
    frame_ok = (global_frames >= 0) & (global_frames < tile_frames * lax.axis_size("frame"))
    row_ids = row_index + offsets
    row_ok = (row_ids >= 0) & (row_ids < lax.axis_size("row"))
    bias_rows = []
    for j in range(tile_frames):
        ok = row_ok[:, None] & frame_ok[None, j : j + 3]
        ok = jnp.broadcast_to(ok[:, :, None], (3, 3, tile_size)).reshape(1, 9 * tile_size)
        bias_rows.append(jnp.where(ok, 0.0, -jnp.inf).astype(jnp.float32))
    bias = jnp.stack(bias_rows)

    q = tiles(query)
    kernel = functools.partial(
        attention_kernel, tile_frames=tile_frames, score_scale=score_scale
    )
    window_block = (3, tile_frames + 2, tile_size, HD)
    out = pl.pallas_call(
        kernel,
        grid=(heads_here,),
        in_specs=[
            pl.BlockSpec((tile_frames, 1, 9 * tile_size), lambda h: (0, 0, 0)),
            pl.BlockSpec((tile_frames, tile_size, HD), lambda h: (0, 0, h)),
            pl.BlockSpec(window_block, lambda h: (0, 0, 0, h)),
            pl.BlockSpec(window_block, lambda h: (0, 0, 0, h)),
        ],
        out_specs=pl.BlockSpec((tile_frames, tile_size, HD), lambda h: (0, 0, h)),
        out_shape=jax.ShapeDtypeStruct(q.shape, query.dtype),
        compiler_params=pltpu.CompilerParams(vmem_limit_bytes=48 * 1024 * 1024),
    )(bias, q, key_window, value_window)
    return out.reshape(frames, rows, columns, features)


def solution(mesh):
    return jax.shard_map(
        per_device,
        mesh=mesh,
        in_specs=(
            P(("clips", "frame"), "row", None, "head"),
            P(("clips", "frame"), "row", None, "head"),
            P(("clips", "frame"), "row", None, "head"),
        ),
        out_specs=P(("clips", "frame"), "row", None, "head"),
        check_vma=False,
    )
```

```python
import functools
import math

import jax
import jax.numpy as jnp
from jax import lax
from jax.experimental import pallas as pl
from jax.experimental.pallas import tpu as pltpu
from jax.sharding import PartitionSpec as P

HD = 128
TF = 4
TR = 8
TC = 8


def shift(cells, axis, forward):
    count = lax.axis_size(axis)
    if forward:
        pairs = [(i, i + 1) for i in range(count - 1)]
    else:
        pairs = [(i + 1, i) for i in range(count - 1)]
    return lax.ppermute(cells, axis, pairs)


def attention_kernel(bias_ref, q_ref, k_ref, v_ref, o_ref, *, tile_frames, score_scale):
    for j in range(tile_frames):
        q = q_ref[j]
        k = k_ref[:, j : j + 3].reshape(-1, HD)
        v = v_ref[:, j : j + 3].reshape(-1, HD)
        s = lax.dot_general(q, k, (((1,), (1,)), ((), ())), preferred_element_type=jnp.float32)
        s = s * score_scale + bias_ref[j]
        m = jnp.max(s, axis=1, keepdims=True)
        p = jnp.exp(s - m)
        l = jnp.sum(p, axis=1, keepdims=True)
        o = jnp.dot(p.astype(jnp.bfloat16), v, preferred_element_type=jnp.float32)
        o_ref[j] = (o / l).astype(o_ref.dtype)


def per_device(query, keys, values):
    frames, rows, columns, features = query.shape
    tile_frames = frames // TF
    tile_size = TF * TR * TC
    heads_here = features // HD
    score_scale = 1.0 / math.sqrt(HD)

    def tiles(x):
        return x.reshape(tile_frames, tile_size, features)

    frame_count = lax.axis_size("frame")
    row_count = lax.axis_size("row")
    kv = jnp.stack((tiles(keys), tiles(values)))
    above = [shift(kv[:, t], "row", True) for t in range(tile_frames)]
    below = [shift(kv[:, t], "row", False) for t in range(tile_frames)]
    own_prev = shift(kv[:, tile_frames - 1], "frame", True)
    own_next = shift(kv[:, 0], "frame", False)

    def diagonal(cells, forward, holders):
        pairs = []
        for f in range(frame_count - 1):
            for r in holders:
                pair = (f * row_count + r, (f + 1) * row_count + r)
                pairs.append(pair if forward else pair[::-1])
        return lax.ppermute(cells, ("frame", "row"), pairs)

    top_prev = diagonal(above[-1], True, range(1, row_count))
    top_next = diagonal(above[0], False, range(1, row_count))
    bottom_prev = diagonal(below[-1], True, range(row_count - 1))
    bottom_next = diagonal(below[0], False, range(row_count - 1))

    def band(prev, middle, following):
        return jnp.stack([prev] + middle + [following], 1)

    kv_window = jnp.stack(
        (
            band(top_prev, above, top_next),
            band(own_prev, [kv[:, t] for t in range(tile_frames)], own_next),
            band(bottom_prev, below, bottom_next),
        ),
        1,
    )

    frame_index = lax.axis_index("frame")
    row_index = lax.axis_index("row")
    offsets = jnp.arange(3, dtype=jnp.int32) - 1
    global_frames = frame_index * tile_frames + jnp.arange(tile_frames + 2, dtype=jnp.int32) - 1
    frame_ok = (global_frames >= 0) & (global_frames < tile_frames * lax.axis_size("frame"))
    row_ids = row_index + offsets
    row_ok = (row_ids >= 0) & (row_ids < lax.axis_size("row"))
    bias_rows = []
    for j in range(tile_frames):
        ok = row_ok[:, None] & frame_ok[None, j : j + 3]
        ok = jnp.broadcast_to(ok[:, :, None], (3, 3, tile_size)).reshape(1, 9 * tile_size)
        bias_rows.append(jnp.where(ok, 0.0, -jnp.inf).astype(jnp.float32))
    bias = jnp.stack(bias_rows)

    q = tiles(query)
    kernel = functools.partial(
        attention_kernel, tile_frames=tile_frames, score_scale=score_scale
    )
    window_block = (3, tile_frames + 2, tile_size, HD)
    out = pl.pallas_call(
        kernel,
        grid=(heads_here,),
        in_specs=[
            pl.BlockSpec((tile_frames, 1, 9 * tile_size), lambda h: (0, 0, 0)),
            pl.BlockSpec((tile_frames, tile_size, HD), lambda h: (0, 0, h)),
            pl.BlockSpec((None,) + window_block, lambda h: (0, 0, 0, 0, h)),
            pl.BlockSpec((None,) + window_block, lambda h: (1, 0, 0, 0, h)),
        ],
        out_specs=pl.BlockSpec((tile_frames, tile_size, HD), lambda h: (0, 0, h)),
        out_shape=jax.ShapeDtypeStruct(q.shape, query.dtype),
        compiler_params=pltpu.CompilerParams(vmem_limit_bytes=48 * 1024 * 1024),
    )(bias, q, kv_window, kv_window)
    return out.reshape(frames, rows, columns, features)


def solution(mesh):
    return jax.shard_map(
        per_device,
        mesh=mesh,
        in_specs=(
            P(("clips", "frame"), "row", None, "head"),
            P(("clips", "frame"), "row", None, "head"),
            P(("clips", "frame"), "row", None, "head"),
        ),
        out_specs=P(("clips", "frame"), "row", None, "head"),
        check_vma=False,
    )
```

```python
import functools
import math

import jax
import jax.numpy as jnp
from jax import lax
from jax.experimental import pallas as pl
from jax.experimental.pallas import tpu as pltpu
from jax.sharding import PartitionSpec as P

HD = 128
TF = 4
TR = 8
TC = 8


def shift(cells, axis, forward):
    count = lax.axis_size(axis)
    if forward:
        pairs = [(i, i + 1) for i in range(count - 1)]
    else:
        pairs = [(i + 1, i) for i in range(count - 1)]
    return lax.ppermute(cells, axis, pairs)


def attention_kernel(bias_ref, q_ref, k_ref, v_ref, o_ref, *, tile_frames, score_scale):
    for j in range(tile_frames):
        q = q_ref[j]
        k = k_ref[:, j : j + 3].reshape(-1, HD)
        v = v_ref[:, j : j + 3].reshape(-1, HD)
        s = lax.dot_general(q, k, (((1,), (1,)), ((), ())), preferred_element_type=jnp.float32)
        s = s * score_scale + bias_ref[j]
        m = jnp.max(s, axis=1, keepdims=True)
        p = jnp.exp(s - m)
        l = jnp.sum(p, axis=1, keepdims=True)
        o = jnp.dot(p.astype(jnp.bfloat16), v, preferred_element_type=jnp.float32)
        o_ref[j] = (o / l).astype(o_ref.dtype)


def per_device(query, keys, values):
    chunks = 2
    frames, rows, columns, features = query.shape
    width = features // chunks
    parts = [
        chunk_attention(*(x[..., c * width : (c + 1) * width] for x in (query, keys, values)))
        for c in range(chunks)
    ]
    return jnp.concatenate(parts, -1)


def chunk_attention(query, keys, values):
    frames, rows, columns, features = query.shape
    tile_frames = frames // TF
    tile_size = TF * TR * TC
    heads_here = features // HD
    score_scale = 1.0 / math.sqrt(HD)

    def tiles(x):
        return x.reshape(tile_frames, tile_size, features)

    frame_count = lax.axis_size("frame")
    row_count = lax.axis_size("row")
    kv = jnp.stack((tiles(keys), tiles(values)))
    above = [shift(kv[:, t], "row", True) for t in range(tile_frames)]
    below = [shift(kv[:, t], "row", False) for t in range(tile_frames)]
    own_prev = shift(kv[:, tile_frames - 1], "frame", True)
    own_next = shift(kv[:, 0], "frame", False)

    def diagonal(cells, forward, holders):
        pairs = []
        for f in range(frame_count - 1):
            for r in holders:
                pair = (f * row_count + r, (f + 1) * row_count + r)
                pairs.append(pair if forward else pair[::-1])
        return lax.ppermute(cells, ("frame", "row"), pairs)

    top_prev = diagonal(above[-1], True, range(1, row_count))
    top_next = diagonal(above[0], False, range(1, row_count))
    bottom_prev = diagonal(below[-1], True, range(row_count - 1))
    bottom_next = diagonal(below[0], False, range(row_count - 1))

    def band(prev, middle, following):
        return jnp.stack([prev] + middle + [following], 1)

    kv_window = jnp.stack(
        (
            band(top_prev, above, top_next),
            band(own_prev, [kv[:, t] for t in range(tile_frames)], own_next),
            band(bottom_prev, below, bottom_next),
        ),
        1,
    )

    frame_index = lax.axis_index("frame")
    row_index = lax.axis_index("row")
    offsets = jnp.arange(3, dtype=jnp.int32) - 1
    global_frames = frame_index * tile_frames + jnp.arange(tile_frames + 2, dtype=jnp.int32) - 1
    frame_ok = (global_frames >= 0) & (global_frames < tile_frames * lax.axis_size("frame"))
    row_ids = row_index + offsets
    row_ok = (row_ids >= 0) & (row_ids < lax.axis_size("row"))
    bias_rows = []
    for j in range(tile_frames):
        ok = row_ok[:, None] & frame_ok[None, j : j + 3]
        ok = jnp.broadcast_to(ok[:, :, None], (3, 3, tile_size)).reshape(1, 9 * tile_size)
        bias_rows.append(jnp.where(ok, 0.0, -jnp.inf).astype(jnp.float32))
    bias = jnp.stack(bias_rows)

    q = tiles(query)
    kernel = functools.partial(
        attention_kernel, tile_frames=tile_frames, score_scale=score_scale
    )
    window_block = (3, tile_frames + 2, tile_size, HD)
    out = pl.pallas_call(
        kernel,
        grid=(heads_here,),
        in_specs=[
            pl.BlockSpec((tile_frames, 1, 9 * tile_size), lambda h: (0, 0, 0)),
            pl.BlockSpec((tile_frames, tile_size, HD), lambda h: (0, 0, h)),
            pl.BlockSpec((None,) + window_block, lambda h: (0, 0, 0, 0, h)),
            pl.BlockSpec((None,) + window_block, lambda h: (1, 0, 0, 0, h)),
        ],
        out_specs=pl.BlockSpec((tile_frames, tile_size, HD), lambda h: (0, 0, h)),
        out_shape=jax.ShapeDtypeStruct(q.shape, query.dtype),
        compiler_params=pltpu.CompilerParams(vmem_limit_bytes=48 * 1024 * 1024),
    )(bias, q, kv_window, kv_window)
    return out.reshape(frames, rows, columns, features)


def solution(mesh):
    return jax.shard_map(
        per_device,
        mesh=mesh,
        in_specs=(
            P(("clips", "frame"), "row", None, "head"),
            P(("clips", "frame"), "row", None, "head"),
            P(("clips", "frame"), "row", None, "head"),
        ),
        out_specs=P(("clips", "frame"), "row", None, "head"),
        check_vma=False,
    )
```

```python
import functools
import math

import jax
import jax.numpy as jnp
from jax import lax
from jax.experimental import pallas as pl
from jax.experimental.pallas import tpu as pltpu
from jax.sharding import PartitionSpec as P

HD = 128
TF = 4
TR = 8
TC = 8


def shift(cells, axis, forward):
    count = lax.axis_size(axis)
    if forward:
        pairs = [(i, i + 1) for i in range(count - 1)]
    else:
        pairs = [(i + 1, i) for i in range(count - 1)]
    return lax.ppermute(cells, axis, pairs)


def attention_kernel(bias_ref, q_ref, k_ref, v_ref, o_ref, *, tile_frames, score_scale):
    for j in range(tile_frames):
        q = q_ref[j]
        k = k_ref[:, j : j + 3].reshape(-1, HD)
        v = v_ref[:, j : j + 3].reshape(-1, HD)
        s = lax.dot_general(q, k, (((1,), (1,)), ((), ())), preferred_element_type=jnp.float32)
        s = s * score_scale + bias_ref[j]
        m = jnp.max(s, axis=1, keepdims=True)
        p = jnp.exp(s - m)
        l = jnp.sum(p, axis=1, keepdims=True)
        o = jnp.dot(p.astype(jnp.bfloat16), v, preferred_element_type=jnp.float32)
        o_ref[j] = (o / l).astype(o_ref.dtype)


def per_device(query, keys, values):
    chunks = 2
    frames, rows, columns, features = query.shape
    width = features // chunks
    parts = [
        chunk_attention(*(x[..., c * width : (c + 1) * width] for x in (query, keys, values)))
        for c in range(chunks)
    ]
    return jnp.concatenate(parts, -1)


def chunk_attention(query, keys, values):
    frames, rows, columns, features = query.shape
    tile_frames = frames // TF
    tile_size = TF * TR * TC
    heads_here = features // HD
    score_scale = 1.0 / math.sqrt(HD)

    def tiles(x):
        return x.reshape(tile_frames, tile_size, features)

    frame_count = lax.axis_size("frame")
    row_count = lax.axis_size("row")
    kv = jnp.stack((tiles(keys), tiles(values)))
    above_all = shift(kv, "row", True)
    below_all = shift(kv, "row", False)
    above = [above_all[:, t] for t in range(tile_frames)]
    below = [below_all[:, t] for t in range(tile_frames)]
    own_prev = shift(kv[:, tile_frames - 1], "frame", True)
    own_next = shift(kv[:, 0], "frame", False)

    def diagonal(cells, forward, holders):
        pairs = []
        for f in range(frame_count - 1):
            for r in holders:
                pair = (f * row_count + r, (f + 1) * row_count + r)
                pairs.append(pair if forward else pair[::-1])
        return lax.ppermute(cells, ("frame", "row"), pairs)

    top_prev = diagonal(above[-1], True, range(1, row_count))
    top_next = diagonal(above[0], False, range(1, row_count))
    bottom_prev = diagonal(below[-1], True, range(row_count - 1))
    bottom_next = diagonal(below[0], False, range(row_count - 1))

    def band(prev, middle, following):
        return jnp.stack([prev] + middle + [following], 1)

    kv_window = jnp.stack(
        (
            band(top_prev, above, top_next),
            band(own_prev, [kv[:, t] for t in range(tile_frames)], own_next),
            band(bottom_prev, below, bottom_next),
        ),
        1,
    )

    frame_index = lax.axis_index("frame")
    row_index = lax.axis_index("row")
    offsets = jnp.arange(3, dtype=jnp.int32) - 1
    global_frames = frame_index * tile_frames + jnp.arange(tile_frames + 2, dtype=jnp.int32) - 1
    frame_ok = (global_frames >= 0) & (global_frames < tile_frames * lax.axis_size("frame"))
    row_ids = row_index + offsets
    row_ok = (row_ids >= 0) & (row_ids < lax.axis_size("row"))
    bias_rows = []
    for j in range(tile_frames):
        ok = row_ok[:, None] & frame_ok[None, j : j + 3]
        ok = jnp.broadcast_to(ok[:, :, None], (3, 3, tile_size)).reshape(1, 9 * tile_size)
        bias_rows.append(jnp.where(ok, 0.0, -jnp.inf).astype(jnp.float32))
    bias = jnp.stack(bias_rows)

    q = tiles(query)
    kernel = functools.partial(
        attention_kernel, tile_frames=tile_frames, score_scale=score_scale
    )
    window_block = (3, tile_frames + 2, tile_size, HD)
    out = pl.pallas_call(
        kernel,
        grid=(heads_here,),
        in_specs=[
            pl.BlockSpec((tile_frames, 1, 9 * tile_size), lambda h: (0, 0, 0)),
            pl.BlockSpec((tile_frames, tile_size, HD), lambda h: (0, 0, h)),
            pl.BlockSpec((None,) + window_block, lambda h: (0, 0, 0, 0, h)),
            pl.BlockSpec((None,) + window_block, lambda h: (1, 0, 0, 0, h)),
        ],
        out_specs=pl.BlockSpec((tile_frames, tile_size, HD), lambda h: (0, 0, h)),
        out_shape=jax.ShapeDtypeStruct(q.shape, query.dtype),
        compiler_params=pltpu.CompilerParams(vmem_limit_bytes=48 * 1024 * 1024),
    )(bias, q, kv_window, kv_window)
    return out.reshape(frames, rows, columns, features)


def solution(mesh):
    return jax.shard_map(
        per_device,
        mesh=mesh,
        in_specs=(
            P(("clips", "frame"), "row", None, "head"),
            P(("clips", "frame"), "row", None, "head"),
            P(("clips", "frame"), "row", None, "head"),
        ),
        out_specs=P(("clips", "frame"), "row", None, "head"),
        check_vma=False,
    )
```

```python
import functools
import math

import jax
import jax.numpy as jnp
from jax import lax
from jax.experimental import pallas as pl
from jax.experimental.pallas import tpu as pltpu
from jax.sharding import PartitionSpec as P

HD = 128
TF = 4
TR = 8
TC = 8


def shift(cells, axis, forward):
    count = lax.axis_size(axis)
    if forward:
        pairs = [(i, i + 1) for i in range(count - 1)]
    else:
        pairs = [(i + 1, i) for i in range(count - 1)]
    return lax.ppermute(cells, axis, pairs)


def attention_kernel(bias_ref, q_ref, k_ref, v_ref, o_ref, *, tile_frames, score_scale):
    for j in range(tile_frames):
        q = q_ref[j]
        k = k_ref[:, j : j + 3].reshape(-1, HD)
        v = v_ref[:, j : j + 3].reshape(-1, HD)
        s = lax.dot_general(q, k, (((1,), (1,)), ((), ())), preferred_element_type=jnp.float32)
        s = s * score_scale + bias_ref[j]
        m = jnp.max(s, axis=1, keepdims=True)
        p = jnp.exp(s - m)
        l = jnp.sum(p, axis=1, keepdims=True)
        o = jnp.dot(p.astype(jnp.bfloat16), v, preferred_element_type=jnp.float32)
        o_ref[j] = (o / l).astype(o_ref.dtype)


def per_device(query, keys, values):
    chunks = 3
    frames, rows, columns, features = query.shape
    width = features // chunks
    parts = [
        chunk_attention(*(x[..., c * width : (c + 1) * width] for x in (query, keys, values)))
        for c in range(chunks)
    ]
    return jnp.concatenate(parts, -1)


def chunk_attention(query, keys, values):
    frames, rows, columns, features = query.shape
    tile_frames = frames // TF
    tile_size = TF * TR * TC
    heads_here = features // HD
    score_scale = 1.0 / math.sqrt(HD)

    def tiles(x):
        return x.reshape(tile_frames, tile_size, features)

    frame_count = lax.axis_size("frame")
    row_count = lax.axis_size("row")
    kv = jnp.stack((tiles(keys), tiles(values)))
    above = [shift(kv[:, t], "row", True) for t in range(tile_frames)]
    below = [shift(kv[:, t], "row", False) for t in range(tile_frames)]
    own_prev = shift(kv[:, tile_frames - 1], "frame", True)
    own_next = shift(kv[:, 0], "frame", False)

    def diagonal(cells, forward, holders):
        pairs = []
        for f in range(frame_count - 1):
            for r in holders:
                pair = (f * row_count + r, (f + 1) * row_count + r)
                pairs.append(pair if forward else pair[::-1])
        return lax.ppermute(cells, ("frame", "row"), pairs)

    top_prev = diagonal(above[-1], True, range(1, row_count))
    top_next = diagonal(above[0], False, range(1, row_count))
    bottom_prev = diagonal(below[-1], True, range(row_count - 1))
    bottom_next = diagonal(below[0], False, range(row_count - 1))

    def band(prev, middle, following):
        return jnp.stack([prev] + middle + [following], 1)

    kv_window = jnp.stack(
        (
            band(top_prev, above, top_next),
            band(own_prev, [kv[:, t] for t in range(tile_frames)], own_next),
            band(bottom_prev, below, bottom_next),
        ),
        1,
    )

    frame_index = lax.axis_index("frame")
    row_index = lax.axis_index("row")
    offsets = jnp.arange(3, dtype=jnp.int32) - 1
    global_frames = frame_index * tile_frames + jnp.arange(tile_frames + 2, dtype=jnp.int32) - 1
    frame_ok = (global_frames >= 0) & (global_frames < tile_frames * lax.axis_size("frame"))
    row_ids = row_index + offsets
    row_ok = (row_ids >= 0) & (row_ids < lax.axis_size("row"))
    bias_rows = []
    for j in range(tile_frames):
        ok = row_ok[:, None] & frame_ok[None, j : j + 3]
        ok = jnp.broadcast_to(ok[:, :, None], (3, 3, tile_size)).reshape(1, 9 * tile_size)
        bias_rows.append(jnp.where(ok, 0.0, -jnp.inf).astype(jnp.float32))
    bias = jnp.stack(bias_rows)

    q = tiles(query)
    kernel = functools.partial(
        attention_kernel, tile_frames=tile_frames, score_scale=score_scale
    )
    window_block = (3, tile_frames + 2, tile_size, HD)
    out = pl.pallas_call(
        kernel,
        grid=(heads_here,),
        in_specs=[
            pl.BlockSpec((tile_frames, 1, 9 * tile_size), lambda h: (0, 0, 0)),
            pl.BlockSpec((tile_frames, tile_size, HD), lambda h: (0, 0, h)),
            pl.BlockSpec((None,) + window_block, lambda h: (0, 0, 0, 0, h)),
            pl.BlockSpec((None,) + window_block, lambda h: (1, 0, 0, 0, h)),
        ],
        out_specs=pl.BlockSpec((tile_frames, tile_size, HD), lambda h: (0, 0, h)),
        out_shape=jax.ShapeDtypeStruct(q.shape, query.dtype),
        compiler_params=pltpu.CompilerParams(vmem_limit_bytes=48 * 1024 * 1024),
    )(bias, q, kv_window, kv_window)
    return out.reshape(frames, rows, columns, features)


def solution(mesh):
    return jax.shard_map(
        per_device,
        mesh=mesh,
        in_specs=(
            P(("clips", "frame"), "row", None, "head"),
            P(("clips", "frame"), "row", None, "head"),
            P(("clips", "frame"), "row", None, "head"),
        ),
        out_specs=P(("clips", "frame"), "row", None, "head"),
        check_vma=False,
    )
```

```python
import functools
import math

import jax
import jax.numpy as jnp
from jax import lax
from jax.experimental import pallas as pl
from jax.experimental.pallas import tpu as pltpu
from jax.sharding import PartitionSpec as P

HD = 128
TF = 4
TR = 8
TC = 8


def shift(cells, axis, forward):
    count = lax.axis_size(axis)
    if forward:
        pairs = [(i, i + 1) for i in range(count - 1)]
    else:
        pairs = [(i + 1, i) for i in range(count - 1)]
    return lax.ppermute(cells, axis, pairs)


def attention_kernel(bias_ref, q_ref, k_ref, v_ref, o_ref, *, tile_frames, score_scale):
    for j in range(tile_frames):
        q = q_ref[j]
        k = k_ref[:, j : j + 3].reshape(-1, HD)
        v = v_ref[:, j : j + 3].reshape(-1, HD)
        s = lax.dot_general(q, k, (((1,), (1,)), ((), ())), preferred_element_type=jnp.float32)
        s = s * score_scale + bias_ref[j]
        m = jnp.max(s, axis=1, keepdims=True)
        p = jnp.exp(s - m)
        l = jnp.sum(p, axis=1, keepdims=True)
        o = jnp.dot(p.astype(jnp.bfloat16), v, preferred_element_type=jnp.float32)
        o_ref[j] = (o / l).astype(o_ref.dtype)


def per_device(query, keys, values):
    chunks = 2
    frames, rows, columns, features = query.shape
    width = features // chunks
    parts = [
        chunk_attention(*(x[..., c * width : (c + 1) * width] for x in (query, keys, values)))
        for c in range(chunks)
    ]
    return jnp.concatenate(parts, -1)


def chunk_attention(query, keys, values):
    frames, rows, columns, features = query.shape
    tile_frames = frames // TF
    tile_size = TF * TR * TC
    heads_here = features // HD
    score_scale = 1.0 / math.sqrt(HD)

    def tiles(x):
        return x.reshape(tile_frames, tile_size, features)

    frame_count = lax.axis_size("frame")
    row_count = lax.axis_size("row")
    kv = jnp.stack((tiles(keys), tiles(values)))
    above = [shift(kv[:, t], "row", True) for t in range(tile_frames)]
    below = [shift(kv[:, t], "row", False) for t in range(tile_frames)]
    own_prev = shift(kv[:, tile_frames - 1], "frame", True)
    own_next = shift(kv[:, 0], "frame", False)

    def diagonal(cells, forward, holders):
        pairs = []
        for f in range(frame_count - 1):
            for r in holders:
                pair = (f * row_count + r, (f + 1) * row_count + r)
                pairs.append(pair if forward else pair[::-1])
        return lax.ppermute(cells, ("frame", "row"), pairs)

    top_prev = diagonal(above[-1], True, range(1, row_count))
    top_next = diagonal(above[0], False, range(1, row_count))
    bottom_prev = diagonal(below[-1], True, range(row_count - 1))
    bottom_next = diagonal(below[0], False, range(row_count - 1))

    def band(prev, middle, following):
        return jnp.stack([prev] + middle + [following], 1)

    kv_window = jnp.stack(
        (
            band(top_prev, above, top_next),
            band(own_prev, [kv[:, t] for t in range(tile_frames)], own_next),
            band(bottom_prev, below, bottom_next),
        ),
        1,
    )

    frame_index = lax.axis_index("frame")
    row_index = lax.axis_index("row")
    offsets = jnp.arange(3, dtype=jnp.int32) - 1
    global_frames = frame_index * tile_frames + jnp.arange(tile_frames + 2, dtype=jnp.int32) - 1
    frame_ok = (global_frames >= 0) & (global_frames < tile_frames * lax.axis_size("frame"))
    row_ids = row_index + offsets
    row_ok = (row_ids >= 0) & (row_ids < lax.axis_size("row"))
    bias_rows = []
    for j in range(tile_frames):
        ok = row_ok[:, None] & frame_ok[None, j : j + 3]
        ok = jnp.broadcast_to(ok[:, :, None], (3, 3, tile_size)).reshape(1, 9 * tile_size)
        bias_rows.append(jnp.where(ok, 0.0, -jnp.inf).astype(jnp.float32))
    bias = jnp.stack(bias_rows)

    q = tiles(query)
    kernel = functools.partial(
        attention_kernel, tile_frames=tile_frames, score_scale=score_scale
    )
    window_block = (3, tile_frames + 2, tile_size, HD)
    out = pl.pallas_call(
        kernel,
        grid=(heads_here,),
        in_specs=[
            pl.BlockSpec((tile_frames, 1, 9 * tile_size), lambda h: (0, 0, 0)),
            pl.BlockSpec((tile_frames, tile_size, HD), lambda h: (0, 0, h)),
            pl.BlockSpec((None,) + window_block, lambda h: (0, 0, 0, 0, h)),
            pl.BlockSpec((None,) + window_block, lambda h: (1, 0, 0, 0, h)),
        ],
        out_specs=pl.BlockSpec((tile_frames, tile_size, HD), lambda h: (0, 0, h)),
        out_shape=jax.ShapeDtypeStruct(q.shape, query.dtype),
        compiler_params=pltpu.CompilerParams(
            vmem_limit_bytes=48 * 1024 * 1024, allow_input_fusion=[False, False, True, True]
        ),
    )(bias, q, kv_window, kv_window)
    return out.reshape(frames, rows, columns, features)


def solution(mesh):
    return jax.shard_map(
        per_device,
        mesh=mesh,
        in_specs=(
            P(("clips", "frame"), "row", None, "head"),
            P(("clips", "frame"), "row", None, "head"),
            P(("clips", "frame"), "row", None, "head"),
        ),
        out_specs=P(("clips", "frame"), "row", None, "head"),
        check_vma=False,
    )
```
